32 devices in a mesh: ctx: 16 (over z, y, x), kvh: 2 (over core).
Axes of the slice: x: 2, y: 2, z: 4, core: 2. Of those that a mesh axis runs over, the one named last changes fastest.
Arguments:
- queries: bfloat16 [4096, 8192], P('ctx', 'kvh'), may hold values from -180 to 180
- keys: bfloat16 [4096, 1024], P('ctx', 'kvh'), may hold values from -6 to 6
- values: bfloat16 [4096, 1024], P('ctx', 'kvh'), may hold values from -6 to 6
- fwd_out: bfloat16 [4096, 8192], P('ctx', 'kvh'), may hold values from -4 to 4
- log_sum: float32 [64, 4096], P('kvh', 'ctx'), as said below
- out_grad: bfloat16 [4096, 8192], P('ctx', 'kvh'), may hold values from -6 to 6
- seg_ids: int32 [4096], replicated, may hold values from 0 to 3, as said below
- active: int32 [32, 16], P('ctx'), may hold values from 0 to 1, as said below
Outputs:
- grad_queries: bfloat16 [4096, 8192], P('ctx', 'kvh')
- grad_keys: bfloat16 [4096, 1024], P('ctx', 'kvh')
- grad_values: bfloat16 [4096, 1024], P('ctx', 'kvh')
The draws below stay inside these ranges and needn't reach their ends.
Inputs may be any that keep to these rules, and one draw needn't show every extreme that they name: log_sum[h, t] is the logarithm of the sum over allowed u of exp(scores[h, t, u]) for the given queries and keys. `seg_ids`: document ids never fall along the sequence; every document has 1 to 2048 tokens, and one has exactly 2048. `active`: column 0 is 1 in every row; a row has 1 to 12 ones, and the last row exactly 12.
All inputs are finite; a program needn't handle non-finite values.
Results may differ from the reference program's by a relative error of at most 0.0049.
Values may be sent and summed in bfloat16 or wider, within the bound.
No kernel may reach another device: no remote copies, remote signals or barrier semaphores. Data moves between devices by JAX's collectives and lax.ppermute only.
A program may use at most 64 MiB of HBM per device.

```python
import jax
import jax.numpy as jnp
from jax import lax

D_HEAD = 128
QHEADS = 64
KVHEADS = 8
TOK_DEV = 256
BLK = 128
WINBLK = 16
KMAX = 12
TOKENS = 4096
NBLK = 32
N_CTX = 16


def shared_keys(key):
    base = jax.random.truncated_normal(jax.random.fold_in(key, 11), -6.0, 6.0, (TOKENS, KVHEADS * D_HEAD), jnp.float32)
    return base.astype(jnp.float32)


def shared_queries(key):
    base = jax.random.truncated_normal(jax.random.fold_in(key, 23), -6.0, 6.0, (TOKENS, QHEADS * D_HEAD), jnp.float32)
    return base.astype(jnp.float32)


def shared_segments(key):
    count = N_CTX // 4
    spread = 2 * TOK_DEV
    index = jnp.arange(count + 1, dtype=jnp.int32)
    offsets = jax.random.randint(jax.random.fold_in(key, 41), (count + 1,), 1 - spread, spread, dtype=jnp.int32)
    picked = jax.random.randint(jax.random.fold_in(key, 43), (), 1, count - 1, dtype=jnp.int32)
    phase = jax.random.randint(jax.random.fold_in(key, 47), (), 1 - spread, spread, dtype=jnp.int32)
    offsets = jnp.where(index == picked, -spread, offsets)
    offsets = jnp.where(index == picked + 1, spread, offsets)
    offsets = (offsets + phase).astype(jnp.int32)
    offsets = jnp.where((index == 0) | (index == count), 0, offsets)
    bounds = (4 * TOK_DEV * index + offsets).astype(jnp.int32)
    position = jnp.arange(TOKENS, dtype=jnp.int32)
    return jnp.sum((position[:, None] >= bounds[None, 1:count]).astype(jnp.int32), axis=1).astype(jnp.int32)


def shared_active(key):
    counts = jax.random.randint(jax.random.fold_in(key, 5), (NBLK,), 1, KMAX + 1, dtype=jnp.int32)
    counts = counts.at[NBLK - 1].set(KMAX)
    row_keys = jax.random.split(jax.random.fold_in(key, 7), NBLK)
    ranking = jax.vmap(lambda row_key: jax.random.permutation(row_key, WINBLK - 1))(row_keys).astype(jnp.int32)
    chosen = (ranking < (counts - 1)[:, None]).astype(jnp.int32)
    return jnp.concatenate([jnp.ones((NBLK, 1), jnp.int32), chosen], axis=1).astype(jnp.int32)


def draw_keys(key, part):
    return shared_keys(key).astype(jnp.bfloat16)


def draw_queries(key, part):
    return shared_queries(key).astype(jnp.bfloat16)


def draw_seg_ids(key, part):
    return shared_segments(key).astype(jnp.int32)


def draw_active(key, part):
    return shared_active(key).astype(jnp.int32)


def draw_log_sum(key, part):
    per_group = QHEADS // KVHEADS
    factor = D_HEAD ** (-0.5)
    padding = WINBLK * BLK
    query_all = shared_queries(key).astype(jnp.bfloat16).astype(jnp.float32)
    key_all = shared_keys(key).astype(jnp.bfloat16).astype(jnp.float32)
    seg_all = shared_segments(key)
    flags_all = shared_active(key)
    key_pad = jnp.pad(key_all, ((padding, 0), (0, 0)))
    seg_pad = jnp.pad(seg_all, (padding, 0), constant_values=-1)
    within = jnp.arange(BLK, dtype=jnp.int32)
    distance = jnp.arange(WINBLK, dtype=jnp.int32)

    def one_block(query_index):
        key_block = (query_index - distance).astype(jnp.int32)
        usable = jnp.repeat((flags_all[query_index] > 0) & (key_block >= 0), BLK)
        key_rows = ((key_block[:, None] * BLK + within[None, :]).reshape(-1) + padding).astype(jnp.int32)
        key_pos = key_rows - padding
        first_row = (query_index * BLK).astype(jnp.int32)
        query_pos = first_row + within
        query_seg = lax.dynamic_slice_in_dim(seg_all, first_row, BLK, 0)
        allowed = (key_pos[None, :] <= query_pos[:, None]) & (seg_pad[key_rows][None, :] == query_seg[:, None]) & usable[None, :]
        key_heads = key_pad[key_rows].reshape(WINBLK * BLK, KVHEADS, D_HEAD)
        query_heads = lax.dynamic_slice_in_dim(query_all, first_row, BLK, 0).reshape(BLK, KVHEADS, per_group, D_HEAD)
        scores = jnp.einsum('tgjd,ugd->gjtu', query_heads, key_heads) * factor
        row_max = jnp.max(jnp.where(allowed, scores, -1e+30), axis=-1, keepdims=True)
        row_sum = jnp.sum(jnp.exp(jnp.where(allowed, scores - row_max, -1e+30)), axis=-1, keepdims=True)
        return (row_max + jnp.log(row_sum))[..., 0].reshape(QHEADS, BLK)
    blocks_out = lax.map(one_block, jnp.arange(NBLK, dtype=jnp.int32))
    return jnp.transpose(blocks_out, (1, 0, 2)).reshape(QHEADS, TOKENS).astype(jnp.float32)


def block_scale(key, dims, shards, smallest, top_value):
    loudness, own = 1.0, jax.random.fold_in(key, 6)
    for axis_at, shards_of in shards:
        steps = jnp.exp(jax.random.uniform(jax.random.fold_in(own, axis_at), (shards_of,), jnp.float32, smallest / len(shards), top_value / len(shards)))
        loudness = loudness * jnp.repeat(steps, dims[axis_at] // shards_of).reshape([-1 if axis == axis_at else 1 for axis in range(len(dims))])
    return loudness


def scatter_about(stream_key, shape, scale, most, cuts=(), kind=jnp.bfloat16):
    array = scale * jax.random.normal(stream_key, shape, jnp.float32)
    if cuts:
        array = array * block_scale(stream_key, shape, cuts, -0.22, 0.18)
    return jnp.clip(array, -most, most).astype(kind)


def setup_inputs(seed: int = 0) -> dict:
    streams_of = jax.random.split(jax.random.key(seed), 9)
    queries = draw_queries(jax.random.fold_in(streams_of[8], 71), 0)
    keys = draw_keys(jax.random.fold_in(streams_of[8], 71), 0)
    values = scatter_about(streams_of[2], (TOKENS, KVHEADS * D_HEAD), 1.0, 6.0, ((0, 16), (1, 2)))
    fwd_out = scatter_about(streams_of[3], (TOKENS, QHEADS * D_HEAD), 0.5, 4.0, ((0, 16), (1, 2)))
    log_sum = draw_log_sum(jax.random.fold_in(streams_of[8], 71), 0)
    out_grad = scatter_about(streams_of[5], (TOKENS, QHEADS * D_HEAD), 1.0, 6.0, ((0, 16), (1, 2)))
    seg_ids = draw_seg_ids(jax.random.fold_in(streams_of[8], 71), 0)
    active = draw_active(jax.random.fold_in(streams_of[8], 71), 0)
    return {"queries": queries, "keys": keys, "values": values, "fwd_out": fwd_out, "log_sum": log_sum, "out_grad": out_grad, "seg_ids": seg_ids, "active": active}


LOWEST = -1.0e30


def reference(queries, keys, values, fwd_out, log_sum, out_grad, seg_ids, active):
    per_group = QHEADS // KVHEADS
    factor = D_HEAD ** -0.5
    padding = WINBLK * BLK
    window = KMAX * BLK
    key_pad = jnp.pad(keys, ((padding, 0), (0, 0)))
    value_pad = jnp.pad(values, ((padding, 0), (0, 0)))
    seg_pad = jnp.pad(seg_ids, (padding, 0), constant_values=-1)
    within = jnp.arange(BLK, dtype=jnp.int32)

    def one_block(totals, query_index):
        key_total, value_total = totals
        flags = active[query_index]
        chosen = jnp.argsort(1 - flags, stable=True)[:KMAX].astype(jnp.int32)
        in_use = flags[chosen] > 0
        key_block = (query_index - chosen).astype(jnp.int32)
        key_rows = (key_block[:, None] * BLK + within[None, :]).reshape(-1).astype(jnp.int32) + padding
        key_pos = key_rows - padding
        first_row = (query_index * BLK).astype(jnp.int32)
        query_pos = first_row + within
        query_seg = lax.dynamic_slice_in_dim(seg_ids, first_row, BLK, 0)
        usable = jnp.repeat(in_use & (key_block >= 0), BLK)
        allowed = (key_pos[None, :] <= query_pos[:, None]) & (seg_pad[key_rows][None, :] == query_seg[:, None]) & usable[None, :]
        key_heads = key_pad[key_rows].astype(jnp.float32).reshape(window, KVHEADS, D_HEAD)
        value_heads = value_pad[key_rows].astype(jnp.float32).reshape(window, KVHEADS, D_HEAD)
        query_heads = lax.dynamic_slice_in_dim(queries, first_row, BLK, 0).astype(jnp.float32).reshape(BLK, KVHEADS, per_group, D_HEAD)
        grad_heads = lax.dynamic_slice_in_dim(out_grad, first_row, BLK, 0).astype(jnp.float32).reshape(BLK, KVHEADS, per_group, D_HEAD)
        output_heads = lax.dynamic_slice_in_dim(fwd_out, first_row, BLK, 0).astype(jnp.float32).reshape(BLK, KVHEADS, per_group, D_HEAD)
        scores = jnp.einsum("tgjd,ugd->gjtu", query_heads, key_heads) * factor
        log_part = lax.dynamic_slice_in_dim(log_sum, first_row, BLK, 1).reshape(KVHEADS, per_group, BLK)[..., None]
        delta_row = jnp.einsum("tgjd,tgjd->gjt", grad_heads, output_heads)[..., None]
        weights = jnp.exp(jnp.where(allowed, scores - log_part, LOWEST))
        weights_half = lax.optimization_barrier(weights.astype(jnp.bfloat16)).astype(jnp.float32)
        grad_weights = jnp.einsum("tgjd,ugd->gjtu", grad_heads, value_heads)
        grad_scores = lax.optimization_barrier((weights * (grad_weights - delta_row)).astype(jnp.bfloat16)).astype(jnp.float32)
        grad_query = (jnp.einsum("gjtu,ugd->tgjd", grad_scores, key_heads) * factor).reshape(BLK, QHEADS * D_HEAD).astype(jnp.bfloat16)
        key_term = (jnp.einsum("gjtu,tgjd->ugd", grad_scores, query_heads) * factor).reshape(window, KVHEADS * D_HEAD)
        value_term = jnp.einsum("gjtu,tgjd->ugd", weights_half, grad_heads).reshape(window, KVHEADS * D_HEAD)
        return (key_total.at[key_rows].add(key_term), value_total.at[key_rows].add(value_term)), grad_query

    zero_sums = jnp.zeros((TOKENS + padding, KVHEADS * D_HEAD), jnp.float32)
    sums_out, grad_blocks = lax.scan(one_block, (zero_sums, zero_sums), jnp.arange(TOKENS // BLK, dtype=jnp.int32))
    grad_queries = grad_blocks.reshape(TOKENS, QHEADS * D_HEAD)
    grad_keys = sums_out[0][padding:].astype(jnp.bfloat16)
    grad_values = sums_out[1][padding:].astype(jnp.bfloat16)
    return (grad_queries, grad_keys, grad_values)
```

```python
import functools

import jax
import jax.numpy as jnp
from jax import lax
from jax.experimental import pallas as pl
from jax.experimental.pallas import tpu as pltpu
from jax.sharding import PartitionSpec as P

D_HEAD = 128
BLK = 128
WINBLK = 16
LOWEST = -1e30
LOG2E = 1.4426950408889634


NT = (((1,), (1,)), ((), ()))
TN = (((0,), (0,)), ((), ()))


def pair_kernel(chunks, heads, factor, *refs):
    count_ref, list_ref = refs[:2]
    pair_refs = refs[2 : 2 + chunks]
    stat_refs = refs[2 + chunks : 2 + 2 * chunks]
    start_ref, kv_ref, sum_in = refs[2 + 2 * chunks : 5 + 2 * chunks]
    dq_refs = refs[5 + 2 * chunks : 5 + 3 * chunks]
    sum_ref = refs[5 + 3 * chunks]
    q_s, g_s, l_s, t_s, bias_s, p_s, s_s, dq_s = refs[6 + 3 * chunks :]
    blocks = pair_refs[0].shape[1] // BLK
    if sum_in is None:
        sum_ref[...] = jnp.zeros_like(sum_ref)
    else:
        sum_ref[...] = sum_in[...]
    wide = 2 * BLK
    for chunk in range(chunks):

        def one_block(part, carry, chunk=chunk):
            row = chunk * blocks + part
            rows = pl.ds(pl.multiple_of(part * BLK, BLK), BLK)
            for head in range(heads):
                cols = pl.ds(head * D_HEAD, D_HEAD)
                out = pl.ds(head * BLK, BLK)
                q_s[out, :] = pair_refs[chunk][0, rows, cols]
                g_s[out, :] = pair_refs[chunk][1, rows, cols]
                l_s[0:1, out] = stat_refs[chunk][pl.ds(head, 1), rows] * LOG2E
                t_s[0:1, out] = stat_refs[chunk][pl.ds(heads + head, 1), rows]
            dq_s[...] = jnp.zeros_like(dq_s)
            key_at = lax.broadcasted_iota(jnp.int32, (BLK, BLK), 0)
            query_at = lax.broadcasted_iota(jnp.int32, (BLK, BLK), 1)
            start_row = start_ref[pl.ds(row, 1), :]

            def one_pair(index, inner):
                code = list_ref[row * WINBLK + index]
                place = code // WINBLK
                distance = code % WINBLK
                keys_at = pl.ds(pl.multiple_of(place * BLK, BLK), BLK)
                key = kv_ref[keys_at, 0:D_HEAD]
                value = kv_ref[keys_at, D_HEAD : 2 * D_HEAD]
                there = key_at - distance * BLK
                allowed = (there <= query_at) & (there >= start_row)
                bias_s[...] = jnp.where(allowed, 0.0, LOWEST)
                for part_at in range(0, heads * BLK, wide):
                    span = pl.ds(part_at, wide)
                    score = lax.dot_general(
                        key, q_s[span, :], NT, preferred_element_type=jnp.float32
                    )
                    grad_w = lax.dot_general(
                        value, g_s[span, :], NT, preferred_element_type=jnp.float32
                    )
                    bias = bias_s[...]
                    bias = jnp.concatenate([bias, bias], axis=1)
                    weight = jnp.exp2(score * (factor * LOG2E) + (bias - l_s[0:1, span]))
                    p_s[:, span] = weight.astype(jnp.bfloat16)
                    s_s[:, span] = (weight * (grad_w - t_s[0:1, span])).astype(jnp.bfloat16)
                weights = p_s[...]
                grads = s_s[...]
                sum_ref[keys_at, D_HEAD : 2 * D_HEAD] += jnp.dot(
                    weights, g_s[...], preferred_element_type=jnp.float32
                )
                sum_ref[keys_at, 0:D_HEAD] += jnp.dot(
                    grads, q_s[...], preferred_element_type=jnp.float32
                )
                dq_s[...] += lax.dot_general(key, grads, TN, preferred_element_type=jnp.float32)
                return inner

            lax.fori_loop(0, count_ref[row], one_pair, 0)
            for head in range(heads):
                turned = jnp.transpose(dq_s[:, head * BLK : (head + 1) * BLK]) * factor
                dq_refs[chunk][rows, pl.ds(head * D_HEAD, D_HEAD)] = turned.astype(jnp.bfloat16)
            return carry

        lax.fori_loop(0, blocks, one_block, 0)


def run_pairs(heads, counts, lists, pairs, stats, starts, kv, sums):
    chunks = len(pairs)
    tokens = pairs[0].shape[1]
    factor = D_HEAD ** (-0.5)
    smem = pl.BlockSpec(memory_space=pltpu.SMEM)
    vmem = pl.BlockSpec(memory_space=pltpu.VMEM)
    operands = [counts, lists, *pairs, *stats, starts, kv]
    specs = [smem, smem] + [vmem] * (2 * chunks + 2)
    aliases = {}
    if sums is not None:
        aliases = {len(operands): chunks}
        operands.append(sums)
        specs.append(vmem)

    def kernel(*refs):
        if sums is None:
            cut = 4 + 2 * chunks
            refs = refs[:cut] + (None,) + refs[cut:]
        pair_kernel(chunks, heads, factor, *refs)

    bf16, f32 = jnp.bfloat16, jnp.float32
    results = pl.pallas_call(
        kernel,
        out_shape=[jax.ShapeDtypeStruct((tokens, heads * D_HEAD), bf16)] * chunks
        + [jax.ShapeDtypeStruct((kv.shape[0], 2 * D_HEAD), f32)],
        in_specs=specs,
        out_specs=[vmem] * (chunks + 1),
        scratch_shapes=[
            pltpu.VMEM((heads * BLK, D_HEAD), bf16),
            pltpu.VMEM((heads * BLK, D_HEAD), bf16),
            pltpu.VMEM((8, heads * BLK), f32),
            pltpu.VMEM((8, heads * BLK), f32),
            pltpu.VMEM((BLK, BLK), f32),
            pltpu.VMEM((BLK, heads * BLK), bf16),
            pltpu.VMEM((BLK, heads * BLK), bf16),
            pltpu.VMEM((D_HEAD, heads * BLK), f32),
        ],
        input_output_aliases=aliases,
        compiler_params=pltpu.CompilerParams(vmem_limit_bytes=48 << 20),
        cost_estimate=pl.CostEstimate(
            flops=10 * chunks * tokens * heads * D_HEAD * 6 * BLK,
            bytes_accessed=8 << 20,
            transcendentals=chunks * tokens * heads * 6 * BLK,
        ),
    )(*operands)
    return results[:chunks], results[chunks]


def body(queries, keys, values, fwd_out, log_sum, out_grad, seg_ids, active):
    count = lax.axis_size("ctx")
    device = lax.axis_index("ctx")
    tokens = queries.shape[0]
    groups = keys.shape[1] // D_HEAD
    heads = queries.shape[1] // D_HEAD // groups
    span = heads * D_HEAD
    blocks = tokens // BLK
    plane_blocks = blocks * groups
    back = WINBLK // plane_blocks
    me = device % groups
    plane = device // groups

    def swap(value, mask):
        if mask == 0:
            return value
        return lax.ppermute(value, "ctx", [(s, s ^ mask) for s in range(count)])

    def shift(value, steps):
        moves = [(s, s + steps) for s in range(count) if 0 <= s + steps < count]
        return lax.ppermute(value, "ctx", moves)

    def columns(array, group, width):
        return lax.dynamic_slice_in_dim(array, group * width, width, 1)

    kv_parts = []
    for mask in range(groups):
        group = me ^ mask
        both = jnp.concatenate(
            [columns(keys, group, D_HEAD), columns(values, group, D_HEAD)], axis=1
        )
        kv_parts.append(swap(both, mask))
    pairs = []
    for mask in range(groups):
        group = me ^ mask
        both = jnp.stack([columns(queries, group, span), columns(out_grad, group, span)])
        pairs.append(swap(both, mask))
    kv_planes = [jnp.concatenate(kv_parts, axis=0)]
    for _ in range(back):
        kv_planes.append(shift(kv_planes[-1], groups))
    kv = jnp.concatenate(kv_planes[::-1], axis=0)

    delta = jnp.sum(
        out_grad.reshape(tokens, groups * heads, D_HEAD).astype(jnp.float32)
        * fwd_out.reshape(tokens, groups * heads, D_HEAD).astype(jnp.float32),
        axis=2,
    ).T
    flag_rows = jnp.zeros((8, tokens), jnp.float32)
    flag_rows = flag_rows.at[0:blocks, 0:WINBLK].set(active.astype(jnp.float32))
    stats = []
    for mask in range(groups):
        first = (me ^ mask) * heads
        stat = jnp.concatenate(
            [
                lax.dynamic_slice_in_dim(log_sum, first, heads, 0),
                lax.dynamic_slice_in_dim(delta, first, heads, 0),
                flag_rows,
            ],
            axis=0,
        )
        stats.append(swap(stat, mask))

    order = me ^ jnp.arange(groups, dtype=jnp.int32)
    row_at = (order[:, None] * blocks + jnp.arange(blocks, dtype=jnp.int32)).reshape(-1)
    flags = jnp.concatenate([s[2 * heads : 2 * heads + blocks, 0:WINBLK] for s in stats], axis=0)
    distance = jnp.arange(WINBLK, dtype=jnp.int32)
    query_block = plane * plane_blocks + row_at
    key_block = query_block[:, None] - distance[None, :]
    block_seg = seg_ids.reshape(-1, BLK)
    first_seg = block_seg[:, 0][query_block]
    last_seg = block_seg[:, BLK - 1][jnp.maximum(key_block, 0)]
    used = (flags > 0) & (key_block >= 0) & (last_seg >= first_seg[:, None])
    used = used.astype(jnp.int32)
    rank = jnp.sum(
        jnp.where(distance[None, None, :] < distance[None, :, None], used[:, None, :], 0), axis=2
    )
    rel = row_at[:, None] + back * plane_blocks - distance[None, :]
    in_plane = rel % plane_blocks
    place = (
        (rel // plane_blocks) * plane_blocks
        + ((in_plane // blocks) ^ me) * blocks
        + in_plane % blocks
    )
    code = place * WINBLK + distance[None, :]
    hit = (rank[:, None, :] == distance[None, :, None]) & (used[:, None, :] > 0)
    lists = jnp.sum(jnp.where(hit, code[:, None, :], 0), axis=2)
    counts = jnp.sum(used, axis=1)
    query_seg = block_seg[query_block]
    starts = (
        jnp.sum((seg_ids[:, None] < query_seg.reshape(-1)[None, :]).astype(jnp.int32), axis=0)
    ).reshape(-1, BLK) - query_block[:, None] * BLK

    order_of = [(m,) for m in range(groups)]
    grads = [None] * groups
    sums = None
    for members in order_of:
        rows = slice(members[0] * blocks, (members[-1] + 1) * blocks)
        found, sums = run_pairs(
            heads,
            counts[rows],
            lists[rows].reshape(-1),
            [pairs[m] for m in members],
            [stats[m] for m in members],
            starts[rows],
            kv,
            sums,
        )
        for m, value in zip(members, found):
            grads[m] = value

    grad_queries = jnp.zeros(queries.shape, jnp.bfloat16)
    for mask in range(groups):
        grad_queries = lax.dynamic_update_slice_in_dim(
            grad_queries, swap(grads[mask], mask), (me ^ mask) * span, 1
        )

    per_plane = groups * tokens
    total = sums[0:per_plane]
    for step in range(1, back + 1):
        arrived = shift(total.astype(jnp.bfloat16), -groups)
        total = sums[step * per_plane : (step + 1) * per_plane] + arrived.astype(jnp.float32)
    scale = jnp.where(jnp.arange(2 * D_HEAD) < D_HEAD, D_HEAD ** (-0.5), 1.0)
    total = total * scale[None, :].astype(jnp.float32)
    parts = [
        swap(total[m * tokens : (m + 1) * tokens].astype(jnp.bfloat16), m) for m in range(groups)
    ]
    key_cols, value_cols = [], []
    for group in range(groups):
        picked = parts[0]
        for m in range(1, groups):
            picked = jnp.where((me ^ group) == m, parts[m], picked)
        key_cols.append(picked[:, :D_HEAD])
        value_cols.append(picked[:, D_HEAD:])
    return (
        grad_queries,
        jnp.concatenate(key_cols, axis=1),
        jnp.concatenate(value_cols, axis=1),
    )


def solution(mesh):
    placed = (
        P("ctx", "kvh"),
        P("ctx", "kvh"),
        P("ctx", "kvh"),
        P("ctx", "kvh"),
        P("kvh", "ctx"),
        P("ctx", "kvh"),
        P(),
        P("ctx", None),
    )
    return jax.shard_map(
        body,
        mesh=mesh,
        in_specs=placed,
        out_specs=(P("ctx", "kvh"), P("ctx", "kvh"), P("ctx", "kvh")),
        check_vma=False,
    )
```

```python
import functools

import jax
import jax.numpy as jnp
from jax import lax
from jax.experimental import pallas as pl
from jax.experimental.pallas import tpu as pltpu
from jax.sharding import PartitionSpec as P


D_HEAD = 128
BLK = 128
WINBLK = 16
EXTRA = 16
HALVES = 2
LOWEST = -1e30
LOG2E = 1.4426950408889634


NT = (((1,), (1,)), ((), ()))
TN = (((0,), (0,)), ((), ()))
F32, BF16 = jnp.float32, jnp.bfloat16
VMEM = pl.BlockSpec(memory_space=pltpu.VMEM)
SMEM = pl.BlockSpec(memory_space=pltpu.SMEM)
HBM = pl.BlockSpec(memory_space=pltpu.HBM)
ANY = pl.BlockSpec(memory_space=pl.ANY)
LARGE = pltpu.CompilerParams(vmem_limit_bytes=67043328)
SMALL = pltpu.CompilerParams(vmem_limit_bytes=16 << 20)


def kv_pack_kernel(groups, me_ref, key_ref, value_ref, active_ref, *outs):
    tokens = key_ref.shape[0]
    flags = active_ref[...].astype(F32).astype(BF16)
    for mask in range(groups):
        at = pl.ds(pl.multiple_of((me_ref[0] ^ mask) * D_HEAD, D_HEAD), D_HEAD)
        outs[mask][0:tokens, 0:D_HEAD] = key_ref[:, at]
        outs[mask][0:tokens, D_HEAD : 2 * D_HEAD] = value_ref[:, at]
        outs[mask][tokens : tokens + EXTRA, :] = jnp.zeros((EXTRA, 2 * D_HEAD), BF16)
        outs[mask][tokens : tokens + flags.shape[0], 0 : flags.shape[1]] = flags


def pack_kv(groups, me, keys, values, active):
    shape = jax.ShapeDtypeStruct((keys.shape[0] + EXTRA, 2 * D_HEAD), keys.dtype)
    return pl.pallas_call(
        functools.partial(kv_pack_kernel, groups),
        out_shape=[shape] * groups,
        in_specs=[SMEM] + [VMEM] * 3,
        out_specs=[VMEM] * groups,
        compiler_params=LARGE,
    )(me.reshape(1), keys, values, active)


def split_three(value):
    high = value.astype(BF16)
    rest = value - high.astype(F32)
    middle = rest.astype(BF16)
    return high, middle, (rest - middle.astype(F32)).astype(BF16)


def pair_pack_kernel(heads, group_ref, query_ref, grad_ref, fwd_ref, log_ref, out_ref):
    out_ref[0, 0:BLK, :] = query_ref[...]
    out_ref[0, BLK : 2 * BLK, :] = grad_ref[...]
    ones = jnp.ones((8, 2 * D_HEAD), BF16)
    rows = []
    for head in range(heads):
        cols = pl.ds(head * D_HEAD, D_HEAD)
        product = grad_ref[:, cols].astype(F32) * fwd_ref[:, cols].astype(F32)
        high = product.astype(BF16)
        low = (product - high.astype(F32)).astype(BF16)
        both = jnp.concatenate([high, low], axis=1)
        rows.append(lax.dot_general(ones, both, NT, preferred_element_type=F32)[0:1, :])
    pieces = split_three(log_ref[...]) + split_three(jnp.concatenate(rows, axis=0))
    blank = jnp.zeros((heads, heads * D_HEAD - len(pieces) * BLK), BF16)
    out_ref[0, 2 * BLK : 2 * BLK + heads, :] = jnp.concatenate(pieces + (blank,), axis=1)


def pack_pair(group, heads, queries, out_grad, fwd_out, log_sum):
    tokens = queries.shape[0]
    span = heads * D_HEAD
    spec = pl.BlockSpec((BLK, span), lambda i, g: (i, g[0]))
    return pl.pallas_call(
        functools.partial(pair_pack_kernel, heads),
        out_shape=jax.ShapeDtypeStruct((tokens // BLK, 2 * BLK + heads, span), queries.dtype),
        grid_spec=pltpu.PrefetchScalarGridSpec(
            num_scalar_prefetch=1,
            grid=(tokens // BLK,),
            in_specs=[spec, spec, spec, pl.BlockSpec((heads, BLK), lambda i, g: (g[0], i))],
            out_specs=pl.BlockSpec((1, 2 * BLK + heads, span), lambda i, g: (i, 0, 0)),
        ),
        compiler_params=LARGE,
    )(group.reshape(1), queries, out_grad, fwd_out, log_sum)


def finish_kernel(groups, me_ref, *refs):
    refs = list(refs)
    take = lambda n: [refs.pop(0) for _ in range(n)]
    parts, come, grads = take(groups), take(groups), take(groups)
    query_ref, key_ref, value_ref, held, key_s, value_s, in_sem, out_sem = refs
    span = held.shape[2]
    ins = [
        pltpu.make_async_copy(grads[mask], held.at[mask], in_sem.at[mask])
        for mask in range(groups)
    ]
    for copy in ins:
        copy.start()
    for mask in range(groups):
        at = pl.ds(pl.multiple_of((me_ref[0] ^ mask) * D_HEAD, D_HEAD), D_HEAD)
        total = parts[mask][...].astype(F32) + come[mask][...].astype(F32)
        key_s[:, at] = (total[:, 0:D_HEAD] * D_HEAD ** (-0.5)).astype(BF16)
        value_s[:, at] = total[:, D_HEAD : 2 * D_HEAD].astype(BF16)
    outs = [
        pltpu.make_async_copy(key_s, key_ref, out_sem.at[groups]),
        pltpu.make_async_copy(value_s, value_ref, out_sem.at[groups + 1]),
    ]
    for copy in outs:
        copy.start()
    for mask in range(groups):
        at = pl.ds(pl.multiple_of((me_ref[0] ^ mask) * span, span), span)
        ins[mask].wait()
        copy = pltpu.make_async_copy(held.at[mask], query_ref.at[:, at], out_sem.at[mask])
        copy.start()
        outs.append(copy)
    for copy in outs:
        copy.wait()


def finish(groups, me, parts, come, grads):
    tokens, span = grads[0].shape
    small = jax.ShapeDtypeStruct((tokens, groups * D_HEAD), BF16)
    return pl.pallas_call(
        functools.partial(finish_kernel, groups),
        out_shape=[jax.ShapeDtypeStruct((tokens, groups * span), BF16), small, small],
        in_specs=[SMEM] + [VMEM] * (2 * groups) + [ANY] * groups,
        out_specs=[HBM] * 3,
        scratch_shapes=[
            pltpu.VMEM((groups, tokens, span), BF16),
            pltpu.VMEM(small.shape, BF16),
            pltpu.VMEM(small.shape, BF16),
            pltpu.SemaphoreType.DMA((groups,)),
            pltpu.SemaphoreType.DMA((groups + 2,)),
        ],
        compiler_params=SMALL,
    )(me.reshape(1), *parts, *come, *grads)


def add_kernel(own_ref, come_ref, *outs):
    tokens = outs[0].shape[0]
    for at, out_ref in enumerate(outs):
        rows = pl.ds(at * tokens, tokens)
        out_ref[...] = (own_ref[rows, :] + come_ref[rows, :].astype(F32)).astype(BF16)


def add_sums(own, arrived, tokens):
    count = own.shape[0] // tokens
    return pl.pallas_call(
        add_kernel,
        out_shape=[jax.ShapeDtypeStruct((tokens, own.shape[1]), BF16)] * count,
        in_specs=[VMEM] * 2,
        out_specs=[VMEM] * count,
        compiler_params=SMALL,
    )(own, arrived)


def pair_kernel(chunks, places, ends, heads, factor, *refs):
    refs = list(refs)
    take = lambda n: [refs.pop(0) for _ in range(n)]
    count_ref, list_ref = take(2)
    pair_refs = take(chunks)
    (start_ref,) = take(1)
    kv_refs = take(places[-1][0] + 1)
    earlier = take(1)[0] if ends else None
    dq_refs = take(chunks)
    sum_refs = take(len(ends) if ends else 1)
    q_s, g_s, l_s, t_s, bias_s, p_s, s_s, dq_s, kv_s, pair_s, kv_sem, pair_sem = take(12)
    blocks = pair_refs[0].shape[0]
    tokens = blocks * BLK
    pair_copies = [
        pltpu.make_async_copy(pair_refs[c], pair_s.at[c], pair_sem.at[c]) for c in range(chunks)
    ]
    kv_copies = [
        pltpu.make_async_copy(
            kv_refs[ref].at[pl.ds(first, tokens)], kv_s.at[pl.ds(i * tokens, tokens)], kv_sem.at[i]
        )
        for i, (ref, first) in enumerate(places)
    ]
    for copy in pair_copies[:1] + kv_copies + pair_copies[1:]:
        copy.start()
    if ends:
        sum_ref, early_s, sem = take(3)
        early = pltpu.make_async_copy(earlier, early_s, sem)
        early.start()
    else:
        sum_ref = sum_refs[0]
    sum_ref[...] = jnp.zeros_like(sum_ref)
    for copy in kv_copies:
        copy.wait()
    wide = 2 * BLK
    for chunk in range(chunks):
        pair_copies[chunk].wait()

        def one_block(part, carry, chunk=chunk):
            row = chunk * blocks + part
            rows_at = pl.ds(2 * BLK, heads)
            pieces = pair_s[chunk, part, rows_at, 0 : 6 * BLK].astype(F32)
            pieces = [pieces[:, i * BLK : (i + 1) * BLK] for i in range(6)]
            log_rows = pieces[0] + pieces[1] + pieces[2]
            delta_rows = pieces[3] + pieces[4] + pieces[5]
            for head in range(heads):
                cols = pl.ds(head * D_HEAD, D_HEAD)
                out = pl.ds(head * BLK, BLK)
                q_s[out, :] = pair_s[chunk, part, 0:BLK, cols]
                g_s[out, :] = pair_s[chunk, part, BLK : 2 * BLK, cols]
                l_s[0:1, out] = log_rows[head : head + 1, :] * LOG2E
                t_s[0:1, out] = delta_rows[head : head + 1, :]
            dq_s[...] = jnp.zeros_like(dq_s)
            key_at = lax.broadcasted_iota(jnp.int32, (BLK, BLK), 0)
            query_at = lax.broadcasted_iota(jnp.int32, (BLK, BLK), 1)
            start_row = start_ref[pl.ds(row, 1), :]

            def one_pair(index, inner):
                code = list_ref[row * WINBLK + index]
                place = code // WINBLK
                distance = code % WINBLK
                keys_at = pl.ds(pl.multiple_of(place * BLK, BLK), BLK)
                key = kv_s[keys_at, 0:D_HEAD]
                value = kv_s[keys_at, D_HEAD : 2 * D_HEAD]
                there = key_at - distance * BLK
                allowed = (there <= query_at) & (there >= start_row)
                bias_s[...] = jnp.where(allowed, 0.0, LOWEST)
                for part_at in range(0, heads * BLK, wide):
                    span = pl.ds(part_at, wide)
                    score = lax.dot_general(key, q_s[span, :], NT, preferred_element_type=F32)
                    grad_w = lax.dot_general(value, g_s[span, :], NT, preferred_element_type=F32)
                    bias = bias_s[...]
                    bias = jnp.concatenate([bias, bias], axis=1)
                    weight = jnp.exp2(score * (factor * LOG2E) + (bias - l_s[0:1, span]))
                    p_s[:, span] = weight.astype(BF16)
                    s_s[:, span] = (weight * (grad_w - t_s[0:1, span])).astype(BF16)
                weights = p_s[...]
                grads = s_s[...]
                sum_ref[keys_at, D_HEAD : 2 * D_HEAD] += jnp.dot(
                    weights, g_s[...], preferred_element_type=F32
                )
                sum_ref[keys_at, 0:D_HEAD] += jnp.dot(
                    grads, q_s[...], preferred_element_type=F32
                )
                dq_s[...] += lax.dot_general(key, grads, TN, preferred_element_type=F32)
                return inner

            lax.fori_loop(0, count_ref[row], one_pair, 0)
            for head in range(heads):
                turned = jnp.transpose(dq_s[:, head * BLK : (head + 1) * BLK]) * factor
                dq_refs[chunk][
                    pl.ds(pl.multiple_of(part * BLK, BLK), BLK), pl.ds(head * D_HEAD, D_HEAD)
                ] = turned.astype(BF16)
            return carry

        lax.fori_loop(0, blocks, one_block, 0)
    if ends:
        early.wait()
        first = 0
        for out_ref in sum_refs:
            at = pl.ds(first, out_ref.shape[0])
            out_ref[...] = (sum_ref[at, :] + early_s[at, :]).astype(out_ref.dtype)
            first += out_ref.shape[0]


def run_pairs(heads, tokens, counts, lists, pairs, starts, kv, places, ends=(), earlier=None):
    chunks = len(pairs)
    factor = D_HEAD ** (-0.5)
    operands = [counts, lists, *pairs, starts, *kv]
    specs = [SMEM] * 2 + [HBM] * chunks + [VMEM] + [HBM] * len(kv)
    total = (len(places) * tokens, 2 * D_HEAD)
    scratch = [
        pltpu.VMEM((heads * BLK, D_HEAD), BF16),
        pltpu.VMEM((heads * BLK, D_HEAD), BF16),
        pltpu.VMEM((8, heads * BLK), F32),
        pltpu.VMEM((8, heads * BLK), F32),
        pltpu.VMEM((BLK, BLK), F32),
        pltpu.VMEM((BLK, heads * BLK), BF16),
        pltpu.VMEM((BLK, heads * BLK), BF16),
        pltpu.VMEM((D_HEAD, heads * BLK), F32),
        pltpu.VMEM(total, BF16),
        pltpu.VMEM((chunks,) + pairs[0].shape, BF16),
        pltpu.SemaphoreType.DMA((len(places),)),
        pltpu.SemaphoreType.DMA((chunks,)),
    ]
    outs = [jax.ShapeDtypeStruct((tokens, heads * D_HEAD), BF16)] * chunks
    if ends:
        operands.append(earlier)
        specs.append(HBM)
        outs += [jax.ShapeDtypeStruct((rows, total[1]), kind) for rows, kind in ends]
        scratch += [pltpu.VMEM(total, F32), pltpu.VMEM(total, F32), pltpu.SemaphoreType.DMA]
    else:
        outs.append(jax.ShapeDtypeStruct(total, F32))
    results = pl.pallas_call(
        functools.partial(pair_kernel, chunks, places, ends, heads, factor),
        out_shape=outs,
        in_specs=specs,
        out_specs=[VMEM] * len(outs),
        scratch_shapes=scratch,
        compiler_params=pltpu.CompilerParams(vmem_limit_bytes=24 << 20),
        cost_estimate=pl.CostEstimate(
            flops=10 * chunks * tokens * heads * D_HEAD * 6 * BLK,
            bytes_accessed=8 << 20,
            transcendentals=chunks * tokens * heads * 6 * BLK,
        ),
    )(*operands)
    return results[:chunks], results[chunks:]


def block_lists(flag_parts, seg_ids, me, plane, groups, blocks, back):
    plane_blocks = blocks * groups
    order = me ^ jnp.arange(groups, dtype=jnp.int32)
    row_at = (order[:, None] * blocks + jnp.arange(blocks, dtype=jnp.int32)).reshape(-1)
    flags = jnp.concatenate(flag_parts, axis=0)
    distance = jnp.arange(WINBLK, dtype=jnp.int32)
    query_block = plane * plane_blocks + row_at
    key_block = query_block[:, None] - distance[None, :]
    block_seg = seg_ids.reshape(-1, BLK)
    first_seg = block_seg[:, 0][query_block]
    last_seg = block_seg[:, BLK - 1][jnp.maximum(key_block, 0)]
    used = (flags > 0) & (key_block >= 0) & (last_seg >= first_seg[:, None])
    used = used.astype(jnp.int32)
    rank = jnp.sum(
        jnp.where(distance[None, None, :] < distance[None, :, None], used[:, None, :], 0), axis=2
    )
    rel = row_at[:, None] + back * plane_blocks - distance[None, :]
    in_plane = rel % plane_blocks
    place = (
        (rel // plane_blocks) * plane_blocks
        + ((in_plane // blocks) ^ me) * blocks
        + in_plane % blocks
    )
    code = place * WINBLK + distance[None, :]
    hit = (rank[:, None, :] == distance[None, :, None]) & (used[:, None, :] > 0)
    lists = jnp.sum(jnp.where(hit, code[:, None, :], 0), axis=2)
    counts = jnp.sum(used, axis=1)
    query_seg = block_seg[query_block]
    starts = (
        jnp.sum((seg_ids[:, None] < query_seg.reshape(-1)[None, :]).astype(jnp.int32), axis=0)
    ).reshape(-1, BLK) - query_block[:, None] * BLK
    return counts, lists, starts


def body(queries, keys, values, fwd_out, log_sum, out_grad, seg_ids, active):
    count = lax.axis_size("ctx")
    device = lax.axis_index("ctx")
    tokens = queries.shape[0]
    groups = keys.shape[1] // D_HEAD
    heads = queries.shape[1] // D_HEAD // groups
    blocks = tokens // BLK
    plane_blocks = blocks * groups
    back = WINBLK // plane_blocks
    me = device % groups
    plane = device // groups
    each = groups // HALVES

    def swap(value, mask):
        if mask == 0:
            return value
        return lax.ppermute(value, "ctx", [(s, s ^ mask) for s in range(count)])

    def shift(value, steps):
        moves = [(s, s + steps) for s in range(count) if 0 <= s + steps < count]
        return lax.ppermute(value, "ctx", moves)

    kv_send = pack_kv(groups, me, keys, values, active)
    kv_own = [swap(kv_send[mask], mask) for mask in range(groups)]
    pairs = []
    for mask in range(groups):
        sent = pack_pair(me ^ mask, heads, queries, out_grad, fwd_out, log_sum)
        pairs.append(swap(sent, mask))
    hops = [
        [
            jnp.concatenate([kv_own[h * each + i] for i in range(each)], axis=0)
            for h in range(HALVES)
        ]
    ]
    for _ in range(back):
        hops.append([shift(hops[-1][h], groups) for h in range(HALVES)])
    kv = [half for hop in hops[:0:-1] for half in hop] + kv_own
    places = [(i // each, (i % each) * (tokens + EXTRA)) for i in range(back * groups)]
    places += [(back * HALVES + m, 0) for m in range(groups)]

    counts, lists, starts = block_lists(
        [k[tokens : tokens + blocks, 0:WINBLK] for k in kv_own],
        seg_ids,
        me,
        plane,
        groups,
        blocks,
        back,
    )

    def members_run(members, ends, earlier):
        rows = slice(members[0] * blocks, (members[-1] + 1) * blocks)
        return run_pairs(
            heads,
            tokens,
            counts[rows],
            lists[rows].reshape(-1),
            [pairs[m] for m in members],
            starts[rows],
            kv,
            places,
            ends,
            earlier,
        )

    most = tuple(range(groups - 1))
    half = each * tokens
    ends = [(half, BF16)] * HALVES + [(half, F32)] * (back - 1) * HALVES
    ends += [(tokens, F32)] + [(tokens, BF16)] * (groups - 1)
    grads, sums = members_run(most, (), None)
    last, sums = members_run((groups - 1,), tuple(ends), sums[0])
    grads = list(grads) + list(last)

    parts = [swap(sums[back * HALVES + m], m) for m in range(groups)]
    come = [None] * groups
    for h in range(HALVES):
        sent = sums[h]
        for hop in range(1, back):
            arrived = shift(sent, -groups)
            sent = add_sums(sums[hop * HALVES + h], arrived, tokens)
        for i, m in enumerate(range(h * each, (h + 1) * each)):
            piece = sent[i] if back > 1 else sent[i * tokens : (i + 1) * tokens]
            moves = [(s, (s ^ m) - groups) for s in range(groups, count)]
            come[m] = lax.ppermute(piece, "ctx", moves)
    grads = [swap(grads[mask], mask) for mask in range(groups)]
    return tuple(finish(groups, me, parts, come, grads))


def solution(mesh):
    placed = (
        P("ctx", "kvh"),
        P("ctx", "kvh"),
        P("ctx", "kvh"),
        P("ctx", "kvh"),
        P("kvh", "ctx"),
        P("ctx", "kvh"),
        P(),
        P("ctx", None),
    )
    return jax.shard_map(
        body,
        mesh=mesh,
        in_specs=placed,
        out_specs=(P("ctx", "kvh"), P("ctx", "kvh"), P("ctx", "kvh")),
        check_vma=False,
    )
```

```python
import functools

import jax
import jax.numpy as jnp
from jax import lax
from jax.experimental import pallas as pl
from jax.experimental.pallas import tpu as pltpu
from jax.sharding import PartitionSpec as P


D_HEAD = 128
BLK = 128
WINBLK = 16
EXTRA = 16
HALVES = 2
LOWEST = -1e30
LOG2E = 1.4426950408889634


NT = (((1,), (1,)), ((), ()))
TN = (((0,), (0,)), ((), ()))
F32, BF16 = jnp.float32, jnp.bfloat16
VMEM = pl.BlockSpec(memory_space=pltpu.VMEM)
SMEM = pl.BlockSpec(memory_space=pltpu.SMEM)
HBM = pl.BlockSpec(memory_space=pltpu.HBM)
ANY = pl.BlockSpec(memory_space=pl.ANY)
LARGE = pltpu.CompilerParams(vmem_limit_bytes=67043328)
SMALL = pltpu.CompilerParams(vmem_limit_bytes=16 << 20)


def kv_pack_kernel(groups, me_ref, key_ref, value_ref, active_ref, *outs):
    tokens = key_ref.shape[0]
    flags = active_ref[...].astype(F32).astype(BF16)
    for mask in range(groups):
        at = pl.ds(pl.multiple_of((me_ref[0] ^ mask) * D_HEAD, D_HEAD), D_HEAD)
        outs[mask][0:tokens, 0:D_HEAD] = key_ref[:, at]
        outs[mask][0:tokens, D_HEAD : 2 * D_HEAD] = value_ref[:, at]
        outs[mask][tokens : tokens + EXTRA, :] = jnp.zeros((EXTRA, 2 * D_HEAD), BF16)
        outs[mask][tokens : tokens + flags.shape[0], 0 : flags.shape[1]] = flags


def pack_kv(groups, me, keys, values, active):
    shape = jax.ShapeDtypeStruct((keys.shape[0] + EXTRA, 2 * D_HEAD), keys.dtype)
    return pl.pallas_call(
        functools.partial(kv_pack_kernel, groups),
        out_shape=[shape] * groups,
        in_specs=[SMEM] + [VMEM] * 3,
        out_specs=[VMEM] * groups,
        compiler_params=LARGE,
    )(me.reshape(1), keys, values, active)


def split_three(value):
    high = value.astype(BF16)
    rest = value - high.astype(F32)
    middle = rest.astype(BF16)
    return high, middle, (rest - middle.astype(F32)).astype(BF16)


def pair_pack_kernel(heads, group_ref, query_ref, grad_ref, fwd_ref, log_ref, out_ref):
    out_ref[0, 0:BLK, :] = query_ref[...]
    out_ref[0, BLK : 2 * BLK, :] = grad_ref[...]
    ones = jnp.ones((8, 2 * D_HEAD), BF16)
    rows = []
    for head in range(heads):
        cols = pl.ds(head * D_HEAD, D_HEAD)
        product = grad_ref[:, cols].astype(F32) * fwd_ref[:, cols].astype(F32)
        high = product.astype(BF16)
        low = (product - high.astype(F32)).astype(BF16)
        both = jnp.concatenate([high, low], axis=1)
        rows.append(lax.dot_general(ones, both, NT, preferred_element_type=F32)[0:1, :])
    pieces = split_three(log_ref[...]) + split_three(jnp.concatenate(rows, axis=0))
    blank = jnp.zeros((heads, heads * D_HEAD - len(pieces) * BLK), BF16)
    out_ref[0, 2 * BLK : 2 * BLK + heads, :] = jnp.concatenate(pieces + (blank,), axis=1)


def pack_pair(group, heads, queries, out_grad, fwd_out, log_sum):
    tokens = queries.shape[0]
    span = heads * D_HEAD
    spec = pl.BlockSpec((BLK, span), lambda i, g: (i, g[0]))
    return pl.pallas_call(
        functools.partial(pair_pack_kernel, heads),
        out_shape=jax.ShapeDtypeStruct((tokens // BLK, 2 * BLK + heads, span), queries.dtype),
        grid_spec=pltpu.PrefetchScalarGridSpec(
            num_scalar_prefetch=1,
            grid=(tokens // BLK,),
            in_specs=[spec, spec, spec, pl.BlockSpec((heads, BLK), lambda i, g: (g[0], i))],
            out_specs=pl.BlockSpec((1, 2 * BLK + heads, span), lambda i, g: (i, 0, 0)),
        ),
        compiler_params=LARGE,
    )(group.reshape(1), queries, out_grad, fwd_out, log_sum)


def finish_kernel(groups, me_ref, *refs):
    refs = list(refs)
    take = lambda n: [refs.pop(0) for _ in range(n)]
    parts, come, grads = take(groups), take(groups), take(groups)
    query_ref, key_ref, value_ref, held, key_s, value_s, in_sem, out_sem = refs
    span = held.shape[2]
    ins = [
        pltpu.make_async_copy(grads[mask], held.at[mask], in_sem.at[mask])
        for mask in range(groups)
    ]
    for copy in ins:
        copy.start()
    for mask in range(groups):
        at = pl.ds(pl.multiple_of((me_ref[0] ^ mask) * D_HEAD, D_HEAD), D_HEAD)
        total = parts[mask][...].astype(F32) + come[mask][...].astype(F32)
        key_s[:, at] = (total[:, 0:D_HEAD] * D_HEAD ** (-0.5)).astype(BF16)
        value_s[:, at] = total[:, D_HEAD : 2 * D_HEAD].astype(BF16)
    outs = [
        pltpu.make_async_copy(key_s, key_ref, out_sem.at[groups]),
        pltpu.make_async_copy(value_s, value_ref, out_sem.at[groups + 1]),
    ]
    for copy in outs:
        copy.start()
    for mask in range(groups):
        at = pl.ds(pl.multiple_of((me_ref[0] ^ mask) * span, span), span)
        ins[mask].wait()
        copy = pltpu.make_async_copy(held.at[mask], query_ref.at[:, at], out_sem.at[mask])
        copy.start()
        outs.append(copy)
    for copy in outs:
        copy.wait()


def finish(groups, me, parts, come, grads):
    tokens, span = grads[0].shape
    small = jax.ShapeDtypeStruct((tokens, groups * D_HEAD), BF16)
    return pl.pallas_call(
        functools.partial(finish_kernel, groups),
        out_shape=[jax.ShapeDtypeStruct((tokens, groups * span), BF16), small, small],
        in_specs=[SMEM] + [VMEM] * (2 * groups) + [ANY] * groups,
        out_specs=[HBM] * 3,
        scratch_shapes=[
            pltpu.VMEM((groups, tokens, span), BF16),
            pltpu.VMEM(small.shape, BF16),
            pltpu.VMEM(small.shape, BF16),
            pltpu.SemaphoreType.DMA((groups,)),
            pltpu.SemaphoreType.DMA((groups + 2,)),
        ],
        compiler_params=SMALL,
    )(me.reshape(1), *parts, *come, *grads)


def add_kernel(own_ref, come_ref, *outs):
    tokens = outs[0].shape[0]
    for at, out_ref in enumerate(outs):
        rows = pl.ds(at * tokens, tokens)
        out_ref[...] = (own_ref[rows, :] + come_ref[rows, :].astype(F32)).astype(BF16)


def add_sums(own, arrived, tokens):
    count = own.shape[0] // tokens
    return pl.pallas_call(
        add_kernel,
        out_shape=[jax.ShapeDtypeStruct((tokens, own.shape[1]), BF16)] * count,
        in_specs=[VMEM] * 2,
        out_specs=[VMEM] * count,
        compiler_params=SMALL,
    )(own, arrived)


def pair_kernel(chunks, places, ends, heads, factor, *refs):
    refs = list(refs)
    take = lambda n: [refs.pop(0) for _ in range(n)]
    count_ref, list_ref = take(2)
    pair_refs = take(chunks)
    (start_ref,) = take(1)
    kv_refs = take(places[-1][0] + 1)
    earlier = take(1)[0] if ends else None
    dq_refs = take(chunks)
    sum_refs = take(len(ends) if ends else 1)
    q_s, g_s, l_s, t_s, bias_s, p_s, s_s, dq_s, kv_s, pair_s, kv_sem, pair_sem = take(12)
    blocks = pair_refs[0].shape[0]
    tokens = blocks * BLK
    pair_copies = [
        pltpu.make_async_copy(pair_refs[c], pair_s.at[c], pair_sem.at[c]) for c in range(chunks)
    ]
    kv_copies = [
        pltpu.make_async_copy(
            kv_refs[ref].at[pl.ds(first, tokens)], kv_s.at[pl.ds(i * tokens, tokens)], kv_sem.at[i]
        )
        for i, (ref, first) in enumerate(places)
    ]
    for copy in pair_copies[:1] + kv_copies + pair_copies[1:]:
        copy.start()
    if ends:
        sum_ref, sem = take(2)
        early = pltpu.make_async_copy(earlier, sum_ref, sem)
        early.start()
        early.wait()
    else:
        sum_ref = sum_refs[0]
        sum_ref[...] = jnp.zeros_like(sum_ref)
    for copy in kv_copies:
        copy.wait()
    wide = 2 * BLK
    for chunk in range(chunks):
        pair_copies[chunk].wait()

        def one_block(part, carry, chunk=chunk):
            row = chunk * blocks + part
            rows_at = pl.ds(2 * BLK, heads)
            pieces = pair_s[chunk, part, rows_at, 0 : 6 * BLK].astype(F32)
            pieces = [pieces[:, i * BLK : (i + 1) * BLK] for i in range(6)]
            log_rows = pieces[0] + pieces[1] + pieces[2]
            delta_rows = pieces[3] + pieces[4] + pieces[5]
            for head in range(heads):
                cols = pl.ds(head * D_HEAD, D_HEAD)
                out = pl.ds(head * BLK, BLK)
                q_s[out, :] = pair_s[chunk, part, 0:BLK, cols]
                g_s[out, :] = pair_s[chunk, part, BLK : 2 * BLK, cols]
                l_s[0:1, out] = log_rows[head : head + 1, :] * LOG2E
                t_s[0:1, out] = delta_rows[head : head + 1, :]
            dq_s[...] = jnp.zeros_like(dq_s)
            key_at = lax.broadcasted_iota(jnp.int32, (BLK, BLK), 0)
            query_at = lax.broadcasted_iota(jnp.int32, (BLK, BLK), 1)
            start_row = start_ref[pl.ds(row, 1), :]

            def key_place(index):
                code = list_ref[row * WINBLK + jnp.minimum(index, WINBLK - 1)]
                distance = jnp.where(index < count_ref[row], code % WINBLK, -2)
                there = key_at - distance * BLK
                allowed = (there <= query_at) & (there >= start_row)
                place = pl.ds(pl.multiple_of(code // WINBLK * BLK, BLK), BLK)
                return place, jnp.where(allowed, 0.0, LOWEST)

            def two_blocks(index, inner):
                first, first_bias = key_place(2 * index)
                second, second_bias = key_place(2 * index + 1)
                bias_s[0:BLK, :] = first_bias
                bias_s[BLK : 2 * BLK, :] = second_bias
                key = jnp.concatenate([kv_s[first, 0:D_HEAD], kv_s[second, 0:D_HEAD]], axis=0)
                both = pl.ds(D_HEAD, D_HEAD)
                value = jnp.concatenate([kv_s[first, both], kv_s[second, both]], axis=0)
                for part_at in range(0, heads * BLK, wide):
                    span = pl.ds(part_at, wide)
                    score = lax.dot_general(key, q_s[span, :], NT, preferred_element_type=F32)
                    grad_w = lax.dot_general(value, g_s[span, :], NT, preferred_element_type=F32)
                    bias = bias_s[...]
                    bias = jnp.concatenate([bias, bias], axis=1)
                    weight = jnp.exp2(score * (factor * LOG2E) + (bias - l_s[0:1, span]))
                    p_s[:, span] = weight.astype(BF16)
                    s_s[:, span] = (weight * (grad_w - t_s[0:1, span])).astype(BF16)
                grads = s_s[...]
                value_sum = jnp.dot(p_s[...], g_s[...], preferred_element_type=F32)
                key_sum = jnp.dot(grads, q_s[...], preferred_element_type=F32)
                sum_ref[first, D_HEAD : 2 * D_HEAD] += value_sum[0:BLK]
                sum_ref[first, 0:D_HEAD] += key_sum[0:BLK]
                sum_ref[second, D_HEAD : 2 * D_HEAD] += value_sum[BLK : 2 * BLK]
                sum_ref[second, 0:D_HEAD] += key_sum[BLK : 2 * BLK]
                dq_s[...] += lax.dot_general(key, grads, TN, preferred_element_type=F32)
                return inner

            lax.fori_loop(0, (count_ref[row] + 1) // 2, two_blocks, 0)
            for head in range(heads):
                turned = jnp.transpose(dq_s[:, head * BLK : (head + 1) * BLK]) * factor
                dq_refs[chunk][
                    pl.ds(pl.multiple_of(part * BLK, BLK), BLK), pl.ds(head * D_HEAD, D_HEAD)
                ] = turned.astype(BF16)
            return carry

        lax.fori_loop(0, blocks, one_block, 0)
    if ends:
        first = 0
        for out_ref in sum_refs:
            at = pl.ds(first, out_ref.shape[0])
            out_ref[...] = sum_ref[at, :].astype(out_ref.dtype)
            first += out_ref.shape[0]


def run_pairs(heads, tokens, counts, lists, pairs, starts, kv, places, ends=(), earlier=None):
    chunks = len(pairs)
    factor = D_HEAD ** (-0.5)
    operands = [counts, lists, *pairs, starts, *kv]
    specs = [SMEM] * 2 + [HBM] * chunks + [VMEM] + [HBM] * len(kv)
    total = (len(places) * tokens, 2 * D_HEAD)
    scratch = [
        pltpu.VMEM((heads * BLK, D_HEAD), BF16),
        pltpu.VMEM((heads * BLK, D_HEAD), BF16),
        pltpu.VMEM((8, heads * BLK), F32),
        pltpu.VMEM((8, heads * BLK), F32),
        pltpu.VMEM((2 * BLK, BLK), F32),
        pltpu.VMEM((2 * BLK, heads * BLK), BF16),
        pltpu.VMEM((2 * BLK, heads * BLK), BF16),
        pltpu.VMEM((D_HEAD, heads * BLK), F32),
        pltpu.VMEM(total, BF16),
        pltpu.VMEM((chunks,) + pairs[0].shape, BF16),
        pltpu.SemaphoreType.DMA((len(places),)),
        pltpu.SemaphoreType.DMA((chunks,)),
    ]
    outs = [jax.ShapeDtypeStruct((tokens, heads * D_HEAD), BF16)] * chunks
    if ends:
        operands.append(earlier)
        specs.append(HBM)
        outs += [jax.ShapeDtypeStruct((rows, total[1]), kind) for rows, kind in ends]
        scratch += [pltpu.VMEM(total, F32), pltpu.SemaphoreType.DMA]
    else:
        outs.append(jax.ShapeDtypeStruct(total, F32))
    results = pl.pallas_call(
        functools.partial(pair_kernel, chunks, places, ends, heads, factor),
        out_shape=outs,
        in_specs=specs,
        out_specs=[VMEM] * len(outs),
        scratch_shapes=scratch,
        compiler_params=pltpu.CompilerParams(vmem_limit_bytes=24 << 20),
        cost_estimate=pl.CostEstimate(
            flops=10 * chunks * tokens * heads * D_HEAD * 6 * BLK,
            bytes_accessed=8 << 20,
            transcendentals=chunks * tokens * heads * 6 * BLK,
        ),
    )(*operands)
    return results[:chunks], results[chunks:]


def block_lists(flag_parts, seg_ids, me, plane, groups, blocks, back):
    plane_blocks = blocks * groups
    order = me ^ jnp.arange(groups, dtype=jnp.int32)
    row_at = (order[:, None] * blocks + jnp.arange(blocks, dtype=jnp.int32)).reshape(-1)
    flags = jnp.concatenate(flag_parts, axis=0)
    distance = jnp.arange(WINBLK, dtype=jnp.int32)
    query_block = plane * plane_blocks + row_at
    key_block = query_block[:, None] - distance[None, :]
    block_seg = seg_ids.reshape(-1, BLK)
    first_seg = block_seg[:, 0][query_block]
    last_seg = block_seg[:, BLK - 1][jnp.maximum(key_block, 0)]
    used = (flags > 0) & (key_block >= 0) & (last_seg >= first_seg[:, None])
    used = used.astype(jnp.int32)
    rank = jnp.sum(
        jnp.where(distance[None, None, :] < distance[None, :, None], used[:, None, :], 0), axis=2
    )
    rel = row_at[:, None] + back * plane_blocks - distance[None, :]
    in_plane = rel % plane_blocks
    place = (
        (rel // plane_blocks) * plane_blocks
        + ((in_plane // blocks) ^ me) * blocks
        + in_plane % blocks
    )
    code = place * WINBLK + distance[None, :]
    hit = (rank[:, None, :] == distance[None, :, None]) & (used[:, None, :] > 0)
    lists = jnp.sum(jnp.where(hit, code[:, None, :], 0), axis=2)
    counts = jnp.sum(used, axis=1)
    query_seg = block_seg[query_block]
    starts = (
        jnp.sum((seg_ids[:, None] < query_seg.reshape(-1)[None, :]).astype(jnp.int32), axis=0)
    ).reshape(-1, BLK) - query_block[:, None] * BLK
    return counts, lists, starts


def body(queries, keys, values, fwd_out, log_sum, out_grad, seg_ids, active):
    count = lax.axis_size("ctx")
    device = lax.axis_index("ctx")
    tokens = queries.shape[0]
    groups = keys.shape[1] // D_HEAD
    heads = queries.shape[1] // D_HEAD // groups
    blocks = tokens // BLK
    plane_blocks = blocks * groups
    back = WINBLK // plane_blocks
    me = device % groups
    plane = device // groups
    each = groups // HALVES

    def swap(value, mask):
        if mask == 0:
            return value
        return lax.ppermute(value, "ctx", [(s, s ^ mask) for s in range(count)])

    def shift(value, steps):
        moves = [(s, s + steps) for s in range(count) if 0 <= s + steps < count]
        return lax.ppermute(value, "ctx", moves)

    kv_send = pack_kv(groups, me, keys, values, active)
    kv_own = [swap(kv_send[mask], mask) for mask in range(groups)]
    pairs = []
    for mask in range(groups):
        sent = pack_pair(me ^ mask, heads, queries, out_grad, fwd_out, log_sum)
        pairs.append(swap(sent, mask))
    hops = [
        [
            jnp.concatenate([kv_own[h * each + i] for i in range(each)], axis=0)
            for h in range(HALVES)
        ]
    ]
    for _ in range(back):
        hops.append([shift(hops[-1][h], groups) for h in range(HALVES)])
    kv = [half for hop in hops[:0:-1] for half in hop] + kv_own
    places = [(i // each, (i % each) * (tokens + EXTRA)) for i in range(back * groups)]
    places += [(back * HALVES + m, 0) for m in range(groups)]

    counts, lists, starts = block_lists(
        [k[tokens : tokens + blocks, 0:WINBLK] for k in kv_own],
        seg_ids,
        me,
        plane,
        groups,
        blocks,
        back,
    )

    def members_run(members, ends, earlier):
        rows = slice(members[0] * blocks, (members[-1] + 1) * blocks)
        return run_pairs(
            heads,
            tokens,
            counts[rows],
            lists[rows].reshape(-1),
            [pairs[m] for m in members],
            starts[rows],
            kv,
            places,
            ends,
            earlier,
        )

    most = tuple(range(groups - 1))
    half = each * tokens
    ends = [(half, BF16)] * HALVES + [(half, F32)] * (back - 1) * HALVES
    ends += [(tokens, F32)] + [(tokens, BF16)] * (groups - 1)
    grads, sums = members_run(most, (), None)
    last, sums = members_run((groups - 1,), tuple(ends), sums[0])
    grads = list(grads) + list(last)

    parts = [swap(sums[back * HALVES + m], m) for m in range(groups)]
    come = [None] * groups
    for h in range(HALVES):
        sent = sums[h]
        for hop in range(1, back):
            arrived = shift(sent, -groups)
            sent = add_sums(sums[hop * HALVES + h], arrived, tokens)
        for i, m in enumerate(range(h * each, (h + 1) * each)):
            piece = sent[i] if back > 1 else sent[i * tokens : (i + 1) * tokens]
            moves = [(s, (s ^ m) - groups) for s in range(groups, count)]
            come[m] = lax.ppermute(piece, "ctx", moves)
    grads = [swap(grads[mask], mask) for mask in range(groups)]
    return tuple(finish(groups, me, parts, come, grads))


def solution(mesh):
    placed = (
        P("ctx", "kvh"),
        P("ctx", "kvh"),
        P("ctx", "kvh"),
        P("ctx", "kvh"),
        P("kvh", "ctx"),
        P("ctx", "kvh"),
        P(),
        P("ctx", None),
    )
    return jax.shard_map(
        body,
        mesh=mesh,
        in_specs=placed,
        out_specs=(P("ctx", "kvh"), P("ctx", "kvh"), P("ctx", "kvh")),
        check_vma=False,
    )
```

```python
import functools

import jax
import jax.numpy as jnp
from jax import lax
from jax.experimental import pallas as pl
from jax.experimental.pallas import tpu as pltpu
from jax.sharding import PartitionSpec as P


D_HEAD = 128
BLK = 128
WINBLK = 16
EXTRA = 16
HALVES = 2
LOWEST = -1e30
LOG2E = 1.4426950408889634


NT = (((1,), (1,)), ((), ()))
TN = (((0,), (0,)), ((), ()))
F32, BF16 = jnp.float32, jnp.bfloat16
VMEM = pl.BlockSpec(memory_space=pltpu.VMEM)
SMEM = pl.BlockSpec(memory_space=pltpu.SMEM)
HBM = pl.BlockSpec(memory_space=pltpu.HBM)
ANY = pl.BlockSpec(memory_space=pl.ANY)
LARGE = pltpu.CompilerParams(vmem_limit_bytes=67043328)
SMALL = pltpu.CompilerParams(vmem_limit_bytes=16 << 20)


def kv_pack_kernel(groups, me_ref, key_ref, value_ref, active_ref, *outs):
    tokens = key_ref.shape[0]
    flags = active_ref[...].astype(F32).astype(BF16)
    for mask in range(groups):
        at = pl.ds(pl.multiple_of((me_ref[0] ^ mask) * D_HEAD, D_HEAD), D_HEAD)
        outs[mask][0:tokens, 0:D_HEAD] = key_ref[:, at]
        outs[mask][0:tokens, D_HEAD : 2 * D_HEAD] = value_ref[:, at]
        outs[mask][tokens : tokens + EXTRA, :] = jnp.zeros((EXTRA, 2 * D_HEAD), BF16)
        outs[mask][tokens : tokens + flags.shape[0], 0 : flags.shape[1]] = flags


def pack_kv(groups, me, keys, values, active):
    shape = jax.ShapeDtypeStruct((keys.shape[0] + EXTRA, 2 * D_HEAD), keys.dtype)
    return pl.pallas_call(
        functools.partial(kv_pack_kernel, groups),
        out_shape=[shape] * groups,
        in_specs=[SMEM] + [VMEM] * 3,
        out_specs=[VMEM] * groups,
        compiler_params=LARGE,
    )(me.reshape(1), keys, values, active)


def split_three(value):
    high = value.astype(BF16)
    rest = value - high.astype(F32)
    middle = rest.astype(BF16)
    return high, middle, (rest - middle.astype(F32)).astype(BF16)


def pair_pack_kernel(heads, group_ref, query_ref, grad_ref, fwd_ref, log_ref, out_ref):
    out_ref[0, 0:BLK, :] = query_ref[...]
    out_ref[0, BLK : 2 * BLK, :] = grad_ref[...]
    ones = jnp.ones((8, 2 * D_HEAD), BF16)
    rows = []
    for head in range(heads):
        cols = pl.ds(head * D_HEAD, D_HEAD)
        product = grad_ref[:, cols].astype(F32) * fwd_ref[:, cols].astype(F32)
        high = product.astype(BF16)
        low = (product - high.astype(F32)).astype(BF16)
        both = jnp.concatenate([high, low], axis=1)
        rows.append(lax.dot_general(ones, both, NT, preferred_element_type=F32)[0:1, :])
    pieces = split_three(log_ref[...]) + split_three(jnp.concatenate(rows, axis=0))
    blank = jnp.zeros((heads, heads * D_HEAD - len(pieces) * BLK), BF16)
    out_ref[0, 2 * BLK : 2 * BLK + heads, :] = jnp.concatenate(pieces + (blank,), axis=1)


def pack_pair(group, heads, queries, out_grad, fwd_out, log_sum):
    tokens = queries.shape[0]
    span = heads * D_HEAD
    spec = pl.BlockSpec((BLK, span), lambda i, g: (i, g[0]))
    return pl.pallas_call(
        functools.partial(pair_pack_kernel, heads),
        out_shape=jax.ShapeDtypeStruct((tokens // BLK, 2 * BLK + heads, span), queries.dtype),
        grid_spec=pltpu.PrefetchScalarGridSpec(
            num_scalar_prefetch=1,
            grid=(tokens // BLK,),
            in_specs=[spec, spec, spec, pl.BlockSpec((heads, BLK), lambda i, g: (g[0], i))],
            out_specs=pl.BlockSpec((1, 2 * BLK + heads, span), lambda i, g: (i, 0, 0)),
        ),
        compiler_params=LARGE,
    )(group.reshape(1), queries, out_grad, fwd_out, log_sum)


def finish_kernel(groups, me_ref, *refs):
    refs = list(refs)
    take = lambda n: [refs.pop(0) for _ in range(n)]
    parts, come, grads = take(groups), take(groups), take(groups)
    query_ref, key_ref, value_ref, held, key_s, value_s, in_sem, out_sem = refs
    span = held.shape[2]
    ins = [
        pltpu.make_async_copy(grads[mask], held.at[mask], in_sem.at[mask])
        for mask in range(groups)
    ]
    for copy in ins:
        copy.start()
    for mask in range(groups):
        at = pl.ds(pl.multiple_of((me_ref[0] ^ mask) * D_HEAD, D_HEAD), D_HEAD)
        total = parts[mask][...].astype(F32) + come[mask][...].astype(F32)
        key_s[:, at] = (total[:, 0:D_HEAD] * D_HEAD ** (-0.5)).astype(BF16)
        value_s[:, at] = total[:, D_HEAD : 2 * D_HEAD].astype(BF16)
    outs = [
        pltpu.make_async_copy(key_s, key_ref, out_sem.at[groups]),
        pltpu.make_async_copy(value_s, value_ref, out_sem.at[groups + 1]),
    ]
    for copy in outs:
        copy.start()
    for mask in range(groups):
        at = pl.ds(pl.multiple_of((me_ref[0] ^ mask) * span, span), span)
        ins[mask].wait()
        copy = pltpu.make_async_copy(held.at[mask], query_ref.at[:, at], out_sem.at[mask])
        copy.start()
        outs.append(copy)
    for copy in outs:
        copy.wait()


def finish(groups, me, parts, come, grads):
    tokens, span = grads[0].shape
    small = jax.ShapeDtypeStruct((tokens, groups * D_HEAD), BF16)
    return pl.pallas_call(
        functools.partial(finish_kernel, groups),
        out_shape=[jax.ShapeDtypeStruct((tokens, groups * span), BF16), small, small],
        in_specs=[SMEM] + [VMEM] * (2 * groups) + [ANY] * groups,
        out_specs=[HBM] * 3,
        scratch_shapes=[
            pltpu.VMEM((groups, tokens, span), BF16),
            pltpu.VMEM(small.shape, BF16),
            pltpu.VMEM(small.shape, BF16),
            pltpu.SemaphoreType.DMA((groups,)),
            pltpu.SemaphoreType.DMA((groups + 2,)),
        ],
        compiler_params=SMALL,
    )(me.reshape(1), *parts, *come, *grads)


def add_kernel(own_ref, come_ref, *outs):
    tokens = outs[0].shape[0]
    for at, out_ref in enumerate(outs):
        rows = pl.ds(at * tokens, tokens)
        out_ref[...] = (own_ref[rows, :] + come_ref[rows, :].astype(F32)).astype(BF16)


def add_sums(own, arrived, tokens):
    count = own.shape[0] // tokens
    return pl.pallas_call(
        add_kernel,
        out_shape=[jax.ShapeDtypeStruct((tokens, own.shape[1]), BF16)] * count,
        in_specs=[VMEM] * 2,
        out_specs=[VMEM] * count,
        compiler_params=SMALL,
    )(own, arrived)


def pair_kernel(chunks, places, ends, heads, factor, *refs):
    refs = list(refs)
    take = lambda n: [refs.pop(0) for _ in range(n)]
    count_ref, list_ref = take(2)
    pair_refs = take(chunks)
    (start_ref,) = take(1)
    kv_refs = take(places[-1][0] + 1)
    earlier = take(1)[0] if ends else None
    dq_refs = take(chunks)
    sum_refs = take(len(ends) if ends else 1)
    q_s, g_s, l_s, t_s, bias_s, p_s, s_s, dq_s, kv_s, pair_s, kv_sem, pair_sem = take(12)
    blocks = pair_refs[0].shape[0]
    tokens = blocks * BLK
    pair_copies = [
        pltpu.make_async_copy(pair_refs[c], pair_s.at[c], pair_sem.at[c]) for c in range(chunks)
    ]
    kv_copies = [
        pltpu.make_async_copy(
            kv_refs[ref].at[pl.ds(first, tokens)], kv_s.at[pl.ds(i * tokens, tokens)], kv_sem.at[i]
        )
        for i, (ref, first) in enumerate(places)
    ]
    for copy in pair_copies[:1] + kv_copies + pair_copies[1:]:
        copy.start()
    if ends:
        sum_ref, sem = take(2)
        early = pltpu.make_async_copy(earlier, sum_ref, sem)
        early.start()
        early.wait()
    else:
        sum_ref = sum_refs[0]
        sum_ref[...] = jnp.zeros_like(sum_ref)
    for copy in kv_copies:
        copy.wait()
    wide = 2 * BLK
    for chunk in range(chunks):
        pair_copies[chunk].wait()

        def one_block(part, carry, chunk=chunk):
            row = chunk * blocks + part
            rows_at = pl.ds(2 * BLK, heads)
            pieces = pair_s[chunk, part, rows_at, 0 : 6 * BLK].astype(F32)
            pieces = [pieces[:, i * BLK : (i + 1) * BLK] for i in range(6)]
            log_rows = pieces[0] + pieces[1] + pieces[2]
            delta_rows = pieces[3] + pieces[4] + pieces[5]
            for head in range(heads):
                cols = pl.ds(head * D_HEAD, D_HEAD)
                out = pl.ds(head * BLK, BLK)
                q_s[out, :] = pair_s[chunk, part, 0:BLK, cols]
                g_s[out, :] = pair_s[chunk, part, BLK : 2 * BLK, cols]
                l_s[0:1, out] = log_rows[head : head + 1, :] * LOG2E
                t_s[0:1, out] = delta_rows[head : head + 1, :]
            dq_s[...] = jnp.zeros_like(dq_s)
            key_at = lax.broadcasted_iota(jnp.int32, (BLK, BLK), 0)
            query_at = lax.broadcasted_iota(jnp.int32, (BLK, BLK), 1)
            start_row = start_ref[pl.ds(row, 1), :]

            def key_blocks(first, many):
                places = []
                for step in range(many):
                    code = list_ref[row * WINBLK + first + step]
                    there = key_at - code % WINBLK * BLK
                    allowed = (there <= query_at) & (there >= start_row)
                    bias_s[step * BLK : (step + 1) * BLK, :] = jnp.where(allowed, 0.0, LOWEST)
                    places.append(pl.ds(pl.multiple_of(code // WINBLK * BLK, BLK), BLK))
                used = pl.ds(0, many * BLK)
                both = pl.ds(D_HEAD, D_HEAD)
                key = jnp.concatenate([kv_s[at, 0:D_HEAD] for at in places], axis=0)
                value = jnp.concatenate([kv_s[at, both] for at in places], axis=0)
                for part_at in range(0, heads * BLK, wide):
                    span = pl.ds(part_at, wide)
                    score = lax.dot_general(key, q_s[span, :], NT, preferred_element_type=F32)
                    grad_w = lax.dot_general(value, g_s[span, :], NT, preferred_element_type=F32)
                    bias = bias_s[used, :]
                    bias = jnp.concatenate([bias, bias], axis=1)
                    weight = jnp.exp2(score * (factor * LOG2E) + (bias - l_s[0:1, span]))
                    p_s[used, span] = weight.astype(BF16)
                    s_s[used, span] = (weight * (grad_w - t_s[0:1, span])).astype(BF16)
                grads = s_s[used, :]
                value_sum = jnp.dot(p_s[used, :], g_s[...], preferred_element_type=F32)
                key_sum = jnp.dot(grads, q_s[...], preferred_element_type=F32)
                for step, at in enumerate(places):
                    sum_ref[at, both] += value_sum[step * BLK : (step + 1) * BLK]
                    sum_ref[at, 0:D_HEAD] += key_sum[step * BLK : (step + 1) * BLK]
                dq_s[...] += lax.dot_general(key, grads, TN, preferred_element_type=F32)

            def two_blocks(index, inner):
                key_blocks(2 * index, 2)
                return inner

            found = count_ref[row]
            lax.fori_loop(0, found // 2, two_blocks, 0)

            @pl.when(found % 2 == 1)
            def _():
                key_blocks(found - 1, 1)

            for head in range(heads):
                turned = jnp.transpose(dq_s[:, head * BLK : (head + 1) * BLK]) * factor
                dq_refs[chunk][
                    pl.ds(pl.multiple_of(part * BLK, BLK), BLK), pl.ds(head * D_HEAD, D_HEAD)
                ] = turned.astype(BF16)
            return carry

        lax.fori_loop(0, blocks, one_block, 0)
    if ends:
        first = 0
        for out_ref in sum_refs:
            at = pl.ds(first, out_ref.shape[0])
            out_ref[...] = sum_ref[at, :].astype(out_ref.dtype)
            first += out_ref.shape[0]


def run_pairs(heads, tokens, counts, lists, pairs, starts, kv, places, ends=(), earlier=None):
    chunks = len(pairs)
    factor = D_HEAD ** (-0.5)
    operands = [counts, lists, *pairs, starts, *kv]
    specs = [SMEM] * 2 + [HBM] * chunks + [VMEM] + [HBM] * len(kv)
    total = (len(places) * tokens, 2 * D_HEAD)
    scratch = [
        pltpu.VMEM((heads * BLK, D_HEAD), BF16),
        pltpu.VMEM((heads * BLK, D_HEAD), BF16),
        pltpu.VMEM((8, heads * BLK), F32),
        pltpu.VMEM((8, heads * BLK), F32),
        pltpu.VMEM((2 * BLK, BLK), F32),
        pltpu.VMEM((2 * BLK, heads * BLK), BF16),
        pltpu.VMEM((2 * BLK, heads * BLK), BF16),
        pltpu.VMEM((D_HEAD, heads * BLK), F32),
        pltpu.VMEM(total, BF16),
        pltpu.VMEM((chunks,) + pairs[0].shape, BF16),
        pltpu.SemaphoreType.DMA((len(places),)),
        pltpu.SemaphoreType.DMA((chunks,)),
    ]
    outs = [jax.ShapeDtypeStruct((tokens, heads * D_HEAD), BF16)] * chunks
    if ends:
        operands.append(earlier)
        specs.append(HBM)
        outs += [jax.ShapeDtypeStruct((rows, total[1]), kind) for rows, kind in ends]
        scratch += [pltpu.VMEM(total, F32), pltpu.SemaphoreType.DMA]
    else:
        outs.append(jax.ShapeDtypeStruct(total, F32))
    results = pl.pallas_call(
        functools.partial(pair_kernel, chunks, places, ends, heads, factor),
        out_shape=outs,
        in_specs=specs,
        out_specs=[VMEM] * len(outs),
        scratch_shapes=scratch,
        compiler_params=pltpu.CompilerParams(vmem_limit_bytes=24 << 20),
        cost_estimate=pl.CostEstimate(
            flops=10 * chunks * tokens * heads * D_HEAD * 6 * BLK,
            bytes_accessed=8 << 20,
            transcendentals=chunks * tokens * heads * 6 * BLK,
        ),
    )(*operands)
    return results[:chunks], results[chunks:]


def block_lists(flag_parts, seg_ids, me, plane, groups, blocks, back):
    plane_blocks = blocks * groups
    order = me ^ jnp.arange(groups, dtype=jnp.int32)
    row_at = (order[:, None] * blocks + jnp.arange(blocks, dtype=jnp.int32)).reshape(-1)
    flags = jnp.concatenate(flag_parts, axis=0)
    distance = jnp.arange(WINBLK, dtype=jnp.int32)
    query_block = plane * plane_blocks + row_at
    key_block = query_block[:, None] - distance[None, :]
    block_seg = seg_ids.reshape(-1, BLK)
    first_seg = block_seg[:, 0][query_block]
    last_seg = block_seg[:, BLK - 1][jnp.maximum(key_block, 0)]
    used = (flags > 0) & (key_block >= 0) & (last_seg >= first_seg[:, None])
    used = used.astype(jnp.int32)
    rank = jnp.sum(
        jnp.where(distance[None, None, :] < distance[None, :, None], used[:, None, :], 0), axis=2
    )
    rel = row_at[:, None] + back * plane_blocks - distance[None, :]
    in_plane = rel % plane_blocks
    place = (
        (rel // plane_blocks) * plane_blocks
        + ((in_plane // blocks) ^ me) * blocks
        + in_plane % blocks
    )
    code = place * WINBLK + distance[None, :]
    hit = (rank[:, None, :] == distance[None, :, None]) & (used[:, None, :] > 0)
    lists = jnp.sum(jnp.where(hit, code[:, None, :], 0), axis=2)
    counts = jnp.sum(used, axis=1)
    query_seg = block_seg[query_block]
    starts = (
        jnp.sum((seg_ids[:, None] < query_seg.reshape(-1)[None, :]).astype(jnp.int32), axis=0)
    ).reshape(-1, BLK) - query_block[:, None] * BLK
    return counts, lists, starts


def body(queries, keys, values, fwd_out, log_sum, out_grad, seg_ids, active):
    count = lax.axis_size("ctx")
    device = lax.axis_index("ctx")
    tokens = queries.shape[0]
    groups = keys.shape[1] // D_HEAD
    heads = queries.shape[1] // D_HEAD // groups
    blocks = tokens // BLK
    plane_blocks = blocks * groups
    back = WINBLK // plane_blocks
    me = device % groups
    plane = device // groups
    each = groups // HALVES

    def swap(value, mask):
        if mask == 0:
            return value
        return lax.ppermute(value, "ctx", [(s, s ^ mask) for s in range(count)])

    def shift(value, steps):
        moves = [(s, s + steps) for s in range(count) if 0 <= s + steps < count]
        return lax.ppermute(value, "ctx", moves)

    kv_send = pack_kv(groups, me, keys, values, active)
    kv_own = [swap(kv_send[mask], mask) for mask in range(groups)]
    pairs = []
    for mask in range(groups):
        sent = pack_pair(me ^ mask, heads, queries, out_grad, fwd_out, log_sum)
        pairs.append(swap(sent, mask))
    hops = [
        [
            jnp.concatenate([kv_own[h * each + i] for i in range(each)], axis=0)
            for h in range(HALVES)
        ]
    ]
    for _ in range(back):
        hops.append([shift(hops[-1][h], groups) for h in range(HALVES)])
    kv = [half for hop in hops[:0:-1] for half in hop] + kv_own
    places = [(i // each, (i % each) * (tokens + EXTRA)) for i in range(back * groups)]
    places += [(back * HALVES + m, 0) for m in range(groups)]

    counts, lists, starts = block_lists(
        [k[tokens : tokens + blocks, 0:WINBLK] for k in kv_own],
        seg_ids,
        me,
        plane,
        groups,
        blocks,
        back,
    )

    def members_run(members, ends, earlier):
        rows = slice(members[0] * blocks, (members[-1] + 1) * blocks)
        return run_pairs(
            heads,
            tokens,
            counts[rows],
            lists[rows].reshape(-1),
            [pairs[m] for m in members],
            starts[rows],
            kv,
            places,
            ends,
            earlier,
        )

    most = tuple(range(groups - 1))
    half = each * tokens
    ends = [(half, BF16)] * HALVES + [(half, F32)] * (back - 1) * HALVES
    ends += [(tokens, F32)] + [(tokens, BF16)] * (groups - 1)
    grads, sums = members_run(most, (), None)
    last, sums = members_run((groups - 1,), tuple(ends), sums[0])
    grads = list(grads) + list(last)

    parts = [swap(sums[back * HALVES + m], m) for m in range(groups)]
    come = [None] * groups
    for h in range(HALVES):
        sent = sums[h]
        for hop in range(1, back):
            arrived = shift(sent, -groups)
            sent = add_sums(sums[hop * HALVES + h], arrived, tokens)
        for i, m in enumerate(range(h * each, (h + 1) * each)):
            piece = sent[i] if back > 1 else sent[i * tokens : (i + 1) * tokens]
            moves = [(s, (s ^ m) - groups) for s in range(groups, count)]
            come[m] = lax.ppermute(piece, "ctx", moves)
    grads = [swap(grads[mask], mask) for mask in range(groups)]
    return tuple(finish(groups, me, parts, come, grads))


def solution(mesh):
    placed = (
        P("ctx", "kvh"),
        P("ctx", "kvh"),
        P("ctx", "kvh"),
        P("ctx", "kvh"),
        P("kvh", "ctx"),
        P("ctx", "kvh"),
        P(),
        P("ctx", None),
    )
    return jax.shard_map(
        body,
        mesh=mesh,
        in_specs=placed,
        out_specs=(P("ctx", "kvh"), P("ctx", "kvh"), P("ctx", "kvh")),
        check_vma=False,
    )
```
